32 devices in a mesh: dp: 2 (over core), expert: 16 (over z, y, x).
Axes of the slice: x: 2, y: 2, z: 4, core: 2. Of those that a mesh axis runs over, the one named last changes fastest.
Arguments:
- tokens: bfloat16 [4096, 2048], P(('dp', 'expert')), may hold values from -6 to 6
- grad_out: bfloat16 [4096, 2048], P(('dp', 'expert')), may hold values from -6 to 6
- expert_ids: int32 [4096, 4], P(('dp', 'expert')), may hold values from 0 to 15, all different within a row; in each aligned block of 128 rows (0 to 127, 128 to 255, ...) at most 40 rows name the same one
- gate_values: bfloat16 [4096, 4], P(('dp', 'expert')), may hold values from 0.019897461 to 0.796875
- weight_in: bfloat16 [16, 2, 1408, 2048], P('expert', None, 'dp'), may hold values from -0.125 to 0.125
- weight_down: bfloat16 [16, 1408, 2048], P('expert', 'dp'), may hold values from -0.15625 to 0.15625
Outputs:
- grad_tokens: bfloat16 [4096, 2048], P(('dp', 'expert'))
- grad_gates: bfloat16 [4096, 4], P(('dp', 'expert'))
- grad_weight_in: bfloat16 [16, 2, 1408, 2048], P('expert', None, 'dp')
- grad_weight_down: bfloat16 [16, 1408, 2048], P('expert', 'dp')
The draws below stay inside these ranges and needn't reach their ends.
Inputs may be any that keep to these rules, and one draw needn't show every extreme that they name: `expert_ids`: each row names 4 different experts. Within each aligned block of 128 rows (the rows of one device) no expert is named by more than 40 rows, and in some block some expert is named by exactly 40 rows.
All inputs are finite; a program needn't handle non-finite values.
Results may differ from the reference program's by a relative error of at most 0.008.
Values may be sent and summed in bfloat16 or wider, within the bound.
A program may use at most 128 MiB of HBM per device.

```python
import math
import jax
import jax.numpy as jnp
import numpy as np
from jax import lax

D = 2048
FF = 1408
TOP = 4
TOK_DEV = 128
EXPERTS = 16
TOKENS = 4096
CAP = 40
SLOTS = 1280


def block_levels(rng, dims, shards, least, largest):
    level, own = 1.0, jax.random.fold_in(rng, 6)
    for dim, shards_of in shards:
        heights = jnp.exp(jax.random.uniform(jax.random.fold_in(own, dim), (shards_of,), jnp.float32, least / len(shards), largest / len(shards)))
        level = level * jnp.repeat(heights, dims[dim] // shards_of).reshape([-1 if axis == dim else 1 for axis in range(len(dims))])
    return level


def shared_out(stream_key, own, number, rows, amount, top, bound, slope):
    order = jax.random.permutation(stream_key, amount)
    crowded, usual = load_shares(amount, rows * top, bound, slope, True), load_shares(amount, rows * top, bound, slope, False)
    places = jnp.arange(amount)

    def named(sizes, turn):
        used = int((sizes > 0).sum())
        fixed = max(1, used // 4)
        moved = fixed + (places - fixed + turn * (used - fixed)) % max(1, amount - fixed)
        return jnp.zeros((amount,), jnp.int32).at[order[jnp.where(places < fixed, places, moved)]].set(jnp.asarray(sizes, jnp.int32))

    sizes = jnp.where(number % 4 == 0, named(crowded, number // 4), named(usual, number - number // 4 - 1))
    mixed = jax.random.permutation(jax.random.fold_in(own, 3), amount)
    source_of, taker = mixed[0:amount // 2 * 2:2], mixed[1:amount // 2 * 2:2]
    room = jnp.minimum(sizes[source_of] - 1, bound - sizes[taker]) // 2
    room = jnp.where((source_of == order[0]) | (taker == order[0]) | (sizes[taker] == 0), 0, jnp.maximum(room, 0))
    moved = jax.random.randint(jax.random.fold_in(own, 4), (amount // 2,), 0, 1 << 20) % (room + 1)
    sizes = sizes.at[source_of].add(-moved).at[taker].add(moved)
    members = jnp.searchsorted(jnp.cumsum(sizes), jnp.arange(rows * top), side="right").astype(jnp.int32)
    grid = members.reshape(top, rows).T
    grid = grid[jax.random.permutation(jax.random.fold_in(own, 1), rows)]
    turn = jax.random.randint(jax.random.fold_in(own, 2), (rows, 1), 0, top)
    return jnp.take_along_axis(grid, (jnp.arange(top)[None, :] + turn) % top, axis=1)


def load_shares(count, total, limit, lean, full):
    loads = [(1 << 20) // math.isqrt(standing ** lean) + 1 for standing in range(1, count + 1)]
    largest = limit if full else min(limit, max(-(-total // count), total * loads[0] // sum(loads)))
    least = 1 if total - largest >= count - 1 else 0
    holding, spare = [largest] + [least] * (count - 1), total - largest - least * (count - 1)
    while spare > 0:
        movable = [i for i in range(1, count) if holding[i] < largest] or [i for i in range(1, count) if holding[i] < limit]
        mass, budget = sum([loads[i] for i in movable]), spare
        for i in movable:
            extra = min(limit - holding[i], max(1, budget * loads[i] // mass), spare)
            holding[i] = holding[i] + extra
            spare = spare - extra
    return np.array(holding)


def centred(key, shape, deviation, bound, cuts=(), held_as=jnp.bfloat16):
    level = block_levels(key, shape, cuts, -0.22, 0.18) if cuts else 1.0
    values = jax.random.normal(key, shape, jnp.float32) * deviation * level
    return jnp.minimum(jnp.maximum(values, -bound), bound).astype(held_as)


def setup_inputs(seed: int = 0) -> dict:
    splits = jax.random.split(jax.random.key(seed), 7)
    tokens = centred(splits[0], (TOKENS, D), 1.0, 6.0, ((0, 32),))
    grad_out = centred(splits[1], (TOKENS, D), 1.0, 6.0, ((0, 32),))
    expert_ids_keys = jax.random.split(jax.random.fold_in(splits[2], 1), TOKENS // TOK_DEV)
    expert_ids_turns = jax.random.permutation(jax.random.fold_in(splits[2], 3), TOKENS // TOK_DEV)
    expert_ids = jax.vmap(lambda own, number: shared_out(jax.random.fold_in(splits[2], 2), own, number, TOK_DEV, EXPERTS, TOP, CAP, 2))(expert_ids_keys, expert_ids_turns).reshape((TOKENS, TOP))
    gate_values = jnp.clip(jnp.exp(math.log(0.796875) - 3.6901057 * jax.random.uniform(splits[3], (TOKENS, TOP), jnp.float32) ** block_levels(splits[3], (TOKENS, TOP), ((0, 32),), -0.2, 0.2)), 0.019897461, 0.796875).astype(jnp.bfloat16)
    weight_in = centred(splits[4], (EXPERTS, 2, FF, D), D ** -0.5, 0.125, ((0, 16), (2, 2)))
    weight_down = centred(splits[5], (EXPERTS, FF, D), FF ** -0.5, 0.15625, ((0, 16), (1, 2)))
    return {"tokens": tokens, "grad_out": grad_out, "expert_ids": expert_ids, "gate_values": gate_values, "weight_in": weight_in, "weight_down": weight_down}


def expert_grads(inputs_rows, dy_rows, gate_rows, proj_in, proj_down):
    hidden = proj_in.shape[1]
    stacked = proj_in.reshape(2 * hidden, proj_in.shape[2])
    projected = lax.dot_general(inputs_rows, stacked, (((1,), (1,)), ((), ())), preferred_element_type=jnp.float32)
    gate_part = projected[:, :hidden]
    up_part = projected[:, hidden:]
    sigmoid_gate = jax.nn.sigmoid(gate_part)
    silu_gate = gate_part * sigmoid_gate
    hidden_act = (silu_gate * up_part).astype(jnp.bfloat16)
    upstream = lax.dot_general(dy_rows, proj_down, (((1,), (1,)), ((), ())), preferred_element_type=jnp.float32)
    gate_grad = jnp.sum(upstream * hidden_act.astype(jnp.float32), axis=1)
    gate_scale = gate_rows.astype(jnp.float32)[:, None]
    scaled_dy = (gate_scale * dy_rows.astype(jnp.float32)).astype(jnp.bfloat16)
    grad_down = lax.dot_general(hidden_act, scaled_dy, (((0,), (0,)), ((), ())), preferred_element_type=jnp.float32)
    hidden_grad = gate_scale * upstream
    grad_gate_part = (hidden_grad * up_part * sigmoid_gate * (1.0 + gate_part * (1.0 - sigmoid_gate))).astype(jnp.bfloat16)
    grad_up_part = (hidden_grad * silu_gate).astype(jnp.bfloat16)
    joined = jnp.concatenate([grad_gate_part, grad_up_part], axis=1)
    row_grads = jnp.dot(joined, stacked, preferred_element_type=jnp.float32)
    grad_in = lax.dot_general(joined, inputs_rows, (((0,), (0,)), ((), ())), preferred_element_type=jnp.float32)
    return row_grads, gate_grad, grad_in.reshape(2, hidden, proj_in.shape[2]), grad_down


def reference(tokens, grad_out, expert_ids, gate_values, weight_in, weight_down):
    blocks = TOKENS // TOK_DEV
    per_block = TOK_DEV * TOP
    flat_ids = expert_ids.reshape(blocks, per_block)
    onehot = (flat_ids[:, :, None] == jnp.arange(EXPERTS, dtype=jnp.int32)[None, None, :]).astype(jnp.int32)
    running = jnp.cumsum(onehot, axis=1) - 1
    position = jnp.sum(onehot * running, axis=2)
    block_index = jnp.arange(blocks, dtype=jnp.int32)[:, None]
    slot_index = (block_index * CAP + position).reshape(-1).astype(jnp.int32)
    expert_flat = expert_ids.reshape(-1).astype(jnp.int32)
    token_flat = (jnp.arange(TOKENS * TOP, dtype=jnp.int32) // TOP).astype(jnp.int32)
    inputs_lists = jnp.zeros((EXPERTS, SLOTS, D), jnp.bfloat16).at[expert_flat, slot_index].set(tokens[token_flat])
    dy_lists = jnp.zeros((EXPERTS, SLOTS, D), jnp.bfloat16).at[expert_flat, slot_index].set(grad_out[token_flat])
    gate_lists = jnp.zeros((EXPERTS, SLOTS), jnp.bfloat16).at[expert_flat, slot_index].set(gate_values.reshape(-1))

    def one_expert(packed):
        row_grads, gate_grad, grad_in, grad_down = expert_grads(packed[0], packed[1], packed[2], packed[3], packed[4])
        return (row_grads.astype(jnp.bfloat16), gate_grad.astype(jnp.bfloat16), grad_in.astype(jnp.bfloat16), grad_down.astype(jnp.bfloat16))

    row_lists, gate_grads, grad_weight_in, grad_weight_down = lax.map(one_expert, (inputs_lists, dy_lists, gate_lists, weight_in, weight_down))
    picked = row_lists[expert_flat, slot_index].reshape(TOKENS, TOP, D)
    grad_tokens = jnp.sum(picked.astype(jnp.float32), axis=1).astype(jnp.bfloat16)
    grad_gates = gate_grads[expert_flat, slot_index].reshape(TOKENS, TOP)
    return (grad_tokens, grad_gates, grad_weight_in, grad_weight_down)
```

```python
import jax
import jax.numpy as jnp
from jax import lax
from jax.sharding import Mesh, PartitionSpec as P

BF16 = jnp.bfloat16
F32 = jnp.float32
ALL = ("dp", "z", "p")
SWAP = [(0, 1), (1, 0)]
BACK_CHUNKS = 2


def places(member):
    rows = member.shape[-1]
    before = (
        jnp.arange(rows, dtype=jnp.int32)[:, None] < jnp.arange(rows, dtype=jnp.int32)[None, :]
    ).astype(BF16)
    return jnp.einsum("...u,ut->...t", member.astype(BF16), before, preferred_element_type=F32)


def chosen(member, place, capacity):
    slots = jnp.arange(capacity, dtype=jnp.int32).astype(F32)[:, None]
    return member[..., None, :] & (place[..., None, :] == slots)


def hop(value, step, right, nz):
    if right:
        pairs = [(i, i + 1) for i in range(nz - 1) if i <= step]
    else:
        pairs = [(i, i - 1) for i in range(1, nz) if i >= nz - 1 - step]
    return lax.ppermute(value, "z", pairs)


def spread(value, z, nz):
    lefts, rights = [value], [value]
    for k in range(1, nz):
        lefts.append(lax.ppermute(lefts[-1], "z", [(i, i + 1) for i in range(k - 1, nz - 1)]))
        rights.append(lax.ppermute(rights[-1], "z", [(i, i - 1) for i in range(1, nz - k + 1)]))
    blocks = [value] + [jnp.where(z >= m, lefts[m], rights[nz - m]) for m in range(1, nz)]
    return jnp.concatenate(blocks, axis=0), (lefts[-1], rights[-1])


def collect(part, nz):
    from_left = from_right = None
    for step in range(nz - 1):
        go_right, go_left = part[step + 1], part[nz - 1 - step]
        if step:
            go_right = (go_right.astype(F32) + from_left.astype(F32)).astype(BF16)
            go_left = (go_left.astype(F32) + from_right.astype(F32)).astype(BF16)
        from_left = hop(go_right, step, True, nz)
        from_right = hop(go_left, step, False, nz)
    return part[0].astype(F32) + from_left.astype(F32) + from_right.astype(F32)


def body(tokens, grad_out, expert_ids, gate_values, weight_in, weight_down):
    nz, npl = lax.axis_size("z"), lax.axis_size("p")
    z, p = lax.axis_index("z"), lax.axis_index("p")
    experts = nz * npl
    rows, width = tokens.shape
    top = expert_ids.shape[1]
    cap = rows * top * 5 // (4 * experts)
    half = experts * cap
    hidden = weight_down.shape[1]

    tagged = jnp.concatenate(
        [
            tokens,
            expert_ids.astype(BF16),
            gate_values,
            jnp.zeros((rows, 128 - 2 * top), BF16),
        ],
        axis=1,
    )
    tok_col, arrived = spread(tagged, z, nz)
    grad_out, _ = lax.optimization_barrier((grad_out, arrived))
    dy_col, _ = spread(grad_out, z, nz)

    ids_col = tok_col[:, width : width + top].astype(jnp.int32).reshape(nz, rows, top)
    plane = z * npl + jnp.arange(npl, dtype=jnp.int32)
    named = ids_col[None] == plane[:, None, None, None]
    member = jnp.any(named, axis=-1)
    sel = chosen(member, places(member), cap)
    same = jnp.arange(nz)[:, None] == jnp.arange(nz)[None, :]
    pick = (sel[:, :, :, None, :] & same[None, :, None, :, None]).astype(BF16)
    pick = pick.reshape(half, nz * rows)

    def route(col):
        send = jnp.dot(pick, col, preferred_element_type=F32).astype(BF16)
        return lax.all_to_all(
            send.reshape(npl, nz * cap, -1), "p", split_axis=0, concat_axis=0, tiled=True
        ).reshape(half, -1)

    own, dy_col = lax.optimization_barrier((route(tok_col), dy_col))
    far = lax.ppermute(own, "dp", SWAP)
    x = jnp.concatenate([own[:, :width], far[:, :width]], axis=0)
    tags = jnp.concatenate([own[:, width:], far[:, width:]], axis=0)

    mine = tags[:, :top].astype(jnp.int32) == z * npl + p
    g = jnp.sum(jnp.where(mine, tags[:, top : 2 * top].astype(F32), 0.0), axis=1)[:, None]

    w_gate, w_up, w_down = weight_in[0, 0], weight_in[0, 1], weight_down[0]
    w_both = weight_in.reshape(2 * hidden, width)
    across = (((1,), (1,)), ((), ()))
    a = lax.dot_general(x, w_gate, across, preferred_element_type=F32)
    b = lax.dot_general(x, w_up, across, preferred_element_type=F32)
    own_y, a, b = lax.optimization_barrier((route(dy_col), a, b))
    y = jnp.concatenate([own_y, lax.ppermute(own_y, "dp", SWAP)], axis=0)
    sig = jax.nn.sigmoid(a)
    silu = a * sig
    h = (silu * b).astype(BF16)
    u = lax.dot_general(y, w_down, across, preferred_element_type=F32)
    gate_grad = jnp.sum(u * h.astype(F32), axis=1)
    hg = g * u
    da = (hg * b * sig * (1.0 + a * (1.0 - sig))).astype(BF16)
    db = (hg * silu).astype(BF16)
    dab = jnp.concatenate([da, db], axis=1)
    s = (g * y.astype(F32)).astype(BF16)

    inner = (((0,), (0,)), ((), ()))

    high = gate_grad[half:].astype(BF16)
    low = (gate_grad[half:] - high.astype(F32)).astype(BF16)
    outs, weight_grads = [], []
    step = width // BACK_CHUNKS
    for c in range(BACK_CHUNKS):
        w_cols = w_both[:, c * step : (c + 1) * step]
        far_r = jnp.dot(dab[half:], w_cols, preferred_element_type=F32).astype(BF16)
        if c == 0:
            far_r = jnp.concatenate(
                [far_r, high[:, None], low[:, None], jnp.zeros((half, 126), BF16)], axis=1
            )
        came = lax.ppermute(far_r, "dp", SWAP)
        near_r = jnp.dot(dab[:half], w_cols, preferred_element_type=F32)
        r = (near_r + came[:, :step].astype(F32)).astype(BF16)
        if c == 0:
            pg = gate_grad[:half] + came[:, step].astype(F32) + came[:, step + 1].astype(F32)
            r = jnp.concatenate([r, pg.astype(BF16)[:, None], jnp.zeros((half, 127), BF16)], axis=1)
        if c == 0:
            r, lhs, rhs = lax.optimization_barrier((r, dab, x))
        else:
            r, lhs, rhs = lax.optimization_barrier((r, h, s))
        grad_w = lax.dot_general(lhs, rhs, inner, preferred_element_type=F32).astype(BF16)
        back = lax.all_to_all(
            r.reshape(npl, nz * cap, -1), "p", split_axis=0, concat_axis=0, tiled=True
        ).reshape(half, -1)
        back, grad_w = lax.optimization_barrier((back, grad_w))
        weight_grads.append(grad_w)
        part = lax.dot_general(
            pick, back[:, :step], (((0,), (0,)), ((), ())), preferred_element_type=F32
        ).astype(BF16)
        if c == 0:
            slot_pg = back[:, step].astype(F32).reshape(npl, nz, cap)
            row_pg = jnp.sum(jnp.where(sel, slot_pg[..., None], 0.0), axis=2)
            row_pg = jnp.sum(jnp.where(named, row_pg[..., None], 0.0), axis=0)
            row_pg = row_pg.reshape(nz * rows, top).astype(BF16)
            part = jnp.concatenate(
                [part, row_pg, jnp.zeros((nz * rows, 128 - top), BF16)], axis=1
            )
        outs.append(collect(part.reshape(nz, rows, -1), nz))
    grad_gates = outs[0][:, step : step + top].astype(BF16)
    outs[0] = outs[0][:, :step]
    grad_tokens = jnp.concatenate([o.astype(BF16) for o in outs], axis=1)

    gw_in, gw_down = weight_grads
    return grad_tokens, grad_gates, gw_in.reshape(weight_in.shape), gw_down[None]


def solution(mesh):
    nz = 4
    experts = mesh.shape["expert"]
    split = Mesh(
        mesh.devices.reshape(mesh.shape["dp"], nz, experts // nz), ALL
    )
    rows = P(ALL, None)
    w_in = P(("z", "p"), None, "dp", None)
    w_down = P(("z", "p"), "dp", None)
    return jax.shard_map(
        body,
        mesh=split,
        in_specs=(rows, rows, rows, rows, w_in, w_down),
        out_specs=(rows, rows, w_in, w_down),
        check_vma=False,
    )
```
